512 devices in a mesh: stack: 128 (over z, y, core), azimuth: 2 (over x_hi), range: 2 (over x_lo).
Axes of the slice: x: 4 (x_hi: 2, x_lo: 2; x = x_hi * 2 + x_lo), y: 8, z: 8, core: 2. Of those that a mesh axis runs over, the one named last changes fastest.
Arguments:
- phases: bfloat16 [1152, 4, 32768], P('stack', 'azimuth', 'range'), may hold values from -6 to 6
- ifg_pairs: int32 [1152, 2], replicated, may hold values from 0 to 599, as said below
- preconditioner: float32 [600, 600], replicated, as said below
- coherence: int32 [4, 32768], P('azimuth', ('range', 'stack')), may hold values 0 or 1
- geo_tiles: int32 [4, 32768], P('azimuth', ('range', 'stack')), may hold values from 0 to 255, as said below
Outputs:
- deramped: float32 [600, 4, 32768], P(None, 'azimuth', ('range', 'stack'))
The draws below stay inside these ranges and needn't reach their ends.
Inputs may be any that keep to these rules, and one draw needn't show every extreme that they name: `ifg_pairs`: each row names an earlier date first and a later date second. `preconditioner`: a symmetric matrix. geo_tiles[r, c] = min(max(floor((c + shift_r) / 128), 0), 255) with one integer shift_r per slab row, -32 <= shift_r <= 32; some row has shift -32 and another +32.
All inputs are finite; a program needn't handle non-finite values. No bound on the sum of `coherence` on one device may be relied on, other than what follows from the above.
Results may differ from the reference program's by a relative error of at most 0.002.
Values may be sent and summed in bfloat16 or wider, within the bound.
A program may use at most 64 MiB of HBM per device.

```python
import jax
import jax.numpy as jnp
from jax import lax

IFG_COUNT = 1152
DATE_COUNT = 600
REWEIGHTS = 2
COL_DEV = 128
SKEW = 32
SLAB_ROWS = 4
SLAB_COLS = 32768
GEO_TILES = 256


def draw_ifg_pairs(key, part):
    key_start, key_gap = jax.random.split(jax.random.fold_in(key, 11))
    start_date = jax.random.randint(key_start, (IFG_COUNT,), 0, DATE_COUNT)
    gap_days = jax.random.randint(key_gap, (IFG_COUNT,), 1, DATE_COUNT)
    other_date = (start_date + gap_days) % DATE_COUNT
    earlier_date = jnp.minimum(start_date, other_date)
    later_date = jnp.maximum(start_date, other_date)
    row_ids = jnp.arange(IFG_COUNT, dtype=jnp.int32)
    earlier_date = jnp.where(row_ids == 0, 0, earlier_date)
    later_date = jnp.where(row_ids == 0, DATE_COUNT - 1, later_date)
    return jnp.stack([earlier_date, later_date], axis=1).astype(jnp.int32)


def draw_preconditioner(key, part):
    key_diag, key_noise = jax.random.split(jax.random.fold_in(key, 23))
    diagonal = jax.random.uniform(key_diag, (DATE_COUNT,), jnp.float32, 0.04, 0.06)
    noise = jax.random.normal(key_noise, (DATE_COUNT, DATE_COUNT), jnp.float32) * 0.0006
    symmetric = 0.5 * (noise + noise.T)
    return (symmetric + jnp.diag(diagonal)).astype(jnp.float32)


def draw_geo_tiles(key, part):
    row_shift = jax.random.randint(jax.random.fold_in(key, 37), (SLAB_ROWS,), -SKEW, SKEW + 1).astype(jnp.int32)
    row_ids = jnp.arange(SLAB_ROWS, dtype=jnp.int32)
    row_shift = jnp.where(row_ids == 0, -SKEW, row_shift)
    row_shift = jnp.where(row_ids == 1, SKEW, row_shift)
    col_ids = jnp.arange(SLAB_COLS, dtype=jnp.int32)
    tiles = jnp.floor_divide(col_ids[None, :] + row_shift[:, None], COL_DEV)
    return jnp.clip(tiles, 0, GEO_TILES - 1).astype(jnp.int32)


def place_ends(result, key, least, top_value):
    longest = result.shape.index(max(result.shape))
    spots = []
    for shift in (0, 1):
        where = [jax.random.randint(jax.random.fold_in(key, axis), (), 0, length) for axis, length in enumerate(result.shape)]
        where[longest] = (where[longest] + shift) % result.shape[longest]
        spots.append(tuple(where))
    return result.at[spots[0]].set(least).at[spots[1]].set(top_value)


def steps_of(own_key, dims, cuts, least, largest):
    loudness = 1.0
    for position, shards_of in cuts:
        heights = jax.random.uniform(jax.random.fold_in(jax.random.fold_in(own_key, 6), position), (shards_of,), jnp.float32, least / len(cuts), largest / len(cuts))
        loudness = loudness * jnp.repeat(jnp.exp(heights), dims[position] // shards_of).reshape((-1,) + (1,) * (len(dims) - 1 - position))
    return loudness


def gaussian(stream_key, dims, scale, most, cuts=(), kind=jnp.bfloat16):
    level = steps_of(stream_key, dims, cuts, -0.22, 0.18) if cuts else 1.0
    array = jax.random.normal(stream_key, dims, jnp.float32) * scale * level
    return jnp.minimum(jnp.maximum(array, -most), most).astype(kind)


def setup_inputs(seed: int = 0) -> dict:
    streams_of = jax.random.split(jax.random.key(seed), 6)
    return {
        "phases": gaussian(streams_of[0], (IFG_COUNT, SLAB_ROWS, SLAB_COLS), 1.0, 6.0, ((0, 128), (1, 2), (2, 2))),
        "ifg_pairs": draw_ifg_pairs(jax.random.fold_in(streams_of[5], 71), 0),
        "preconditioner": draw_preconditioner(jax.random.fold_in(streams_of[5], 71), 0),
        "coherence": place_ends((jax.random.randint(streams_of[3], (SLAB_ROWS, SLAB_COLS), 0, 4) < 3).astype(jnp.int32), jax.random.fold_in(streams_of[3], 1), 0, 1),
        "geo_tiles": draw_geo_tiles(jax.random.fold_in(streams_of[5], 71), 0),
    }


def plane_solve(gram_matrix, right_side):
    def entry(row_pos, col_pos):
        return gram_matrix[row_pos % 3, col_pos % 3]

    cofactors = [[entry(row_pos + 1, col_pos + 1) * entry(row_pos + 2, col_pos + 2) - entry(row_pos + 1, col_pos + 2) * entry(row_pos + 2, col_pos + 1) for col_pos in range(3)] for row_pos in range(3)]
    determinant = entry(0, 0) * cofactors[0][0] + entry(0, 1) * cofactors[0][1] + entry(0, 2) * cofactors[0][2]
    solution = [(cofactors[0][col_pos] * right_side[0] + cofactors[1][col_pos] * right_side[1] + cofactors[2][col_pos] * right_side[2]) / determinant for col_pos in range(3)]
    return jnp.stack(solution)


def invert_pixels(stack_data, coherence_row, incidence, incidence_half, earlier_date, later_date, preconditioner):
    normal_rhs = lax.dot_general(incidence_half, stack_data, (((0,), (0,)), ((), ())), preferred_element_type=jnp.float32)
    series = jnp.dot(preconditioner, normal_rhs, precision=lax.Precision.HIGHEST, preferred_element_type=jnp.float32)
    values = stack_data.astype(jnp.float32)
    for sweep in range(REWEIGHTS):
        residual = values - (series[later_date] - series[earlier_date])
        square = residual * residual
        robust_scale = jnp.mean(square, axis=0) + 1e-6
        shifted = square + robust_scale
        weight = coherence_row * (robust_scale * robust_scale) / (shifted * shifted)
        update = lax.dot_general(incidence, weight * residual, (((0,), (0,)), ((), ())), precision=lax.Precision.HIGHEST, preferred_element_type=jnp.float32)
        series = series + jnp.dot(preconditioner, update, precision=lax.Precision.HIGHEST, preferred_element_type=jnp.float32)
    return series


def reference(phases, ifg_pairs, preconditioner, coherence, geo_tiles):
    earlier_date = ifg_pairs[:, 0]
    later_date = ifg_pairs[:, 1]
    date_ids = jnp.arange(DATE_COUNT, dtype=jnp.int32)
    incidence = (later_date[:, None] == date_ids).astype(jnp.float32) - (earlier_date[:, None] == date_ids).astype(jnp.float32)
    incidence_half = incidence.astype(jnp.bfloat16)
    block_count = SLAB_COLS // COL_DEV
    row_coord = (jnp.arange(SLAB_ROWS, dtype=jnp.float32) + 0.5) / SLAB_ROWS - 0.5

    def block_basis(block_index):
        col_ids = block_index * COL_DEV + jnp.arange(COL_DEV, dtype=jnp.int32)
        col_coord = (col_ids.astype(jnp.float32) + 0.5) / SLAB_COLS - 0.5
        coord_u = jnp.broadcast_to(row_coord[:, None], (SLAB_ROWS, COL_DEV)).reshape(-1)
        coord_v = jnp.broadcast_to(col_coord[None, :], (SLAB_ROWS, COL_DEV)).reshape(-1)
        coherence_blk = lax.dynamic_slice_in_dim(coherence, block_index * COL_DEV, COL_DEV, 1).reshape(-1).astype(jnp.float32)
        tiles_blk = lax.dynamic_slice_in_dim(geo_tiles, block_index * COL_DEV, COL_DEV, 1).reshape(-1).astype(jnp.int32)
        return coord_u, coord_v, coherence_blk, tiles_blk

    def solve_block(block_index):
        stack_data = lax.dynamic_slice_in_dim(phases, block_index * COL_DEV, COL_DEV, 2).reshape(IFG_COUNT, SLAB_ROWS * COL_DEV)
        coord_u, coord_v, coherence_blk, tiles_blk = block_basis(block_index)
        return invert_pixels(stack_data, coherence_blk, incidence, incidence_half, earlier_date, later_date, preconditioner)

    block_ids = jnp.arange(block_count, dtype=jnp.int32)
    series_blocks = lax.map(solve_block, block_ids)

    def accumulate(totals, block_index):
        moments, gram_matrix = totals
        coord_u, coord_v, coherence_blk, tiles_blk = block_basis(block_index)
        basis = jnp.stack([jnp.ones_like(coord_u), coord_u, coord_v])
        weighted_basis = basis * coherence_blk[None, :]
        series = series_blocks[block_index]
        term = (weighted_basis[:, None, :] * series[None, :, :]).transpose(2, 0, 1)
        moments = moments + jax.ops.segment_sum(term, tiles_blk, num_segments=GEO_TILES)
        products = (weighted_basis[:, None, :] * basis[None, :, :]).transpose(2, 0, 1)
        gram_matrix = gram_matrix + jax.ops.segment_sum(products, tiles_blk, num_segments=GEO_TILES)
        return (moments, gram_matrix), None

    start_totals = (jnp.zeros((GEO_TILES, 3, DATE_COUNT), jnp.float32), jnp.zeros((GEO_TILES, 3, 3), jnp.float32))
    (moments, gram_matrix), unused = lax.scan(accumulate, start_totals, block_ids)
    moments = moments.transpose(1, 2, 0)
    gram_matrix = gram_matrix.transpose(1, 2, 0) + jnp.eye(3, dtype=jnp.float32)[:, :, None]
    plane_coefs = plane_solve(gram_matrix, moments)

    def deramp_block(block_index):
        coord_u, coord_v, coherence_blk, tiles_blk = block_basis(block_index)
        picked = jnp.take(plane_coefs, tiles_blk, axis=2)
        return series_blocks[block_index] - (picked[0] + picked[1] * coord_u + picked[2] * coord_v)

    out_blocks = lax.map(deramp_block, block_ids)
    out_blocks = out_blocks.reshape(block_count, DATE_COUNT, SLAB_ROWS, COL_DEV).transpose(1, 2, 0, 3)
    return out_blocks.reshape(DATE_COUNT, SLAB_ROWS, SLAB_COLS)
```

```python
import functools

import jax
import jax.numpy as jnp
from jax import lax
from jax.experimental import pallas as pl
from jax.experimental.pallas import tpu as pltpu
from jax.sharding import PartitionSpec as P

MESH = pl.DeviceIdType.MESH
F32 = jnp.float32
BF16 = jnp.bfloat16
REWEIGHTS = 2
IFGS = 1152
DATES = 600
DATE_ROWS = 608
DATE_LANES = 640
COLS = 128
ROWS = 2
PIXELS = ROWS * COLS
SLAB_ROWS = 4
SLAB_COLS = 32768
STACK = 128
SIDE = 8
OWN_IFGS = IFGS // STACK
BLOCKS = SLAB_COLS // COLS
REACH = (-2, -1, 0, 1, 2)


def split(value):
    high = value.astype(BF16)
    return high, (value - high.astype(F32)).astype(BF16)


def dot(left, right):
    return jnp.dot(left, right, preferred_element_type=F32)


def ring_hops(step):
    return min(step % SIDE, -step % SIDE)


def far_first():
    steps = [(dz, dy, dc) for dz in range(SIDE) for dy in range(SIDE) for dc in range(2)]
    steps.remove((0, 0, 0))
    return sorted(steps, key=lambda step: -ring_hops(step[0]) - ring_hops(step[1]))


def invert_kernel(
    phases,
    pairs,
    precond,
    coherence,
    tiles,
    series_out,
    moments_out,
    solve_out,
    stacked,
    wide,
    values,
    values_half,
    pairs_v,
    precond_v,
    precond_pad,
    coherence_v,
    tiles_v,
    incidence,
    incidence_t,
    gain_hi,
    gain_lo,
    series,
    series_hi,
    series_lo,
    pull_hi,
    pull_lo,
    gram_own,
    gram_got,
    moments_own,
    moments_got,
    moments_all,
    solve_v,
    load_sem,
    store_sem,
    phase_send,
    phase_recv,
    gram_send,
    gram_recv,
    moment_send,
    moment_recv,
):
    me = lax.axis_index("stack")
    azimuth = lax.axis_index("azimuth")
    block = lax.axis_index("range") * STACK + me
    z, y, core = me // (2 * SIDE), lax.rem(me // 2, SIDE), lax.rem(me, 2)

    def peer(reach, other):
        there = lax.rem(block + reach + BLOCKS, BLOCKS)
        return {
            "stack": lax.rem(there, STACK),
            "azimuth": (1 - azimuth) if other else azimuth,
            "range": there // STACK,
        }

    group = [(reach, other) for other in (0, 1) for reach in REACH if reach or other]

    barrier = pltpu.get_barrier_semaphore()

    def greet(step, carry):
        pl.semaphore_signal(
            barrier, inc=1, device_id={"stack": lax.rem(me + step, STACK)}, device_id_type=MESH
        )
        return carry

    lax.fori_loop(1, STACK, greet, 0)
    for reach, other in group:
        pl.semaphore_signal(barrier, inc=1, device_id=peer(reach, other), device_id_type=MESH)

    small = [
        pltpu.make_async_copy(coherence, coherence_v, load_sem.at[0]),
        pltpu.make_async_copy(tiles, tiles_v, load_sem.at[1]),
        pltpu.make_async_copy(pairs, pairs_v, load_sem.at[2]),
        pltpu.make_async_copy(precond, precond_v, load_sem.at[3]),
        pltpu.make_async_copy(
            phases.at[:, :, pl.ds(pl.multiple_of(me * COLS, COLS), COLS)],
            stacked.at[pl.ds(OWN_IFGS * me, OWN_IFGS)],
            load_sem.at[4],
        ),
    ]
    for copy in small:
        copy.start()

    pl.semaphore_wait(barrier, STACK - 1 + len(group))

    for dz, dy, dc in far_first():
        there = (
            lax.rem(z + dz, SIDE) * (2 * SIDE) + lax.rem(y + dy, SIDE) * 2 + lax.rem(core + dc, 2)
        )
        pltpu.make_async_remote_copy(
            src_ref=phases.at[:, :, pl.ds(pl.multiple_of(there * COLS, COLS), COLS)],
            dst_ref=stacked.at[pl.ds(OWN_IFGS * me, OWN_IFGS)],
            send_sem=phase_send,
            recv_sem=phase_recv,
            device_id={"stack": there},
            device_id_type=MESH,
        ).start()

    small[0].wait()
    small[1].wait()
    coh = coherence_v[...].astype(F32)
    tile_ids = tiles_v[...]
    column = lax.broadcasted_iota(jnp.int32, (1, COLS), 1).astype(F32)
    row_u = [
        ((azimuth * ROWS + row).astype(F32) + 0.5) / SLAB_ROWS - 0.5 for row in range(ROWS)
    ]
    offset_v = [(column - (63.5 + COLS * tile)) / SLAB_COLS for tile in (-1, 0, 1)]
    members = [(tile_ids == block + tile).astype(F32) for tile in (-1, 0, 1)]
    weights = [coh * member for member in members]

    def lanes(pieces):
        return jnp.concatenate(pieces, axis=1)

    basis_rows = []
    for tile in range(3):
        ones = jnp.ones((1, COLS), F32)
        basis_rows.append(
            [
                lanes([ones, ones]),
                lanes([ones * row_u[0], ones * row_u[1]]),
                lanes([offset_v[tile], offset_v[tile]]),
            ]
        )
        w0, w1 = weights[tile][0:1], weights[tile][1:2]
        dv = offset_v[tile]
        both, lean = w0 + w1, w0 * row_u[0] + w1 * row_u[1]
        gram_own[tile] = jnp.concatenate(
            [
                both,
                lean,
                both * dv,
                w0 * (row_u[0] * row_u[0]) + w1 * (row_u[1] * row_u[1]),
                lean * dv,
                both * dv * dv,
                jnp.zeros((2, COLS), F32),
            ],
            axis=0,
        )

    def trade(own, got, send_sem, recv_sem):
        copies = []
        for reach, other in group:
            first, last = max(0, reach), min(3, 3 + reach)
            copies.append(
                pltpu.make_async_remote_copy(
                    src_ref=own.at[pl.ds(first, last - first)],
                    dst_ref=got.at[other, reach + 2, pl.ds(first - reach, last - first)],
                    send_sem=send_sem.at[other, reach + 2],
                    recv_sem=recv_sem.at[other, reach + 2],
                    device_id=peer(reach, other),
                    device_id_type=MESH,
                )
            )
        for copy in copies:
            copy.start()
        return copies

    def gathered(own, got):
        totals = []
        for tile in range(3):
            total = own[tile]
            for reach, other in group:
                if max(0, reach) - reach <= tile < min(3, 3 + reach) - reach:
                    total = total + got[other, reach + 2, tile]
            totals.append(total)
        return totals

    gram_copies = trade(gram_own, gram_got, gram_send, gram_recv)

    small[2].wait()
    earlier, later = pairs_v[0:1, :], pairs_v[1:2, :]
    date_rows = lax.broadcasted_iota(jnp.int32, (DATE_LANES, IFGS), 0)
    incidence_t[...] = (
        jnp.where(later == date_rows, 1.0, 0.0) - jnp.where(earlier == date_rows, 1.0, 0.0)
    ).astype(BF16)
    later_col = jnp.broadcast_to(later.astype(F32), (COLS, IFGS)).T
    earlier_col = jnp.broadcast_to(earlier.astype(F32), (COLS, IFGS)).T
    for part in range(DATE_LANES // 128):
        date_lanes = (
            lax.broadcasted_iota(jnp.int32, (IFGS, 128), 1) + 128 * part
        ).astype(F32)
        incidence[:, 128 * part : 128 * part + 128] = (
            jnp.where(later_col == date_lanes, 1.0, 0.0)
            - jnp.where(earlier_col == date_lanes, 1.0, 0.0)
        ).astype(BF16)
    precond_pad[...] = jnp.zeros((DATE_ROWS, DATE_LANES), F32)
    small[3].wait()
    precond_pad[0:DATES, 0:DATES] = precond_v[...]
    first_hi, first_lo = split(precond_pad[...])
    gain = dot(first_hi, incidence_t[...]) + dot(first_lo, incidence_t[...])
    gain_hi[...], gain_lo[...] = split(gain)
    series_hi[...] = jnp.zeros((DATE_LANES, PIXELS), BF16)
    series_lo[...] = jnp.zeros((DATE_LANES, PIXELS), BF16)

    for copy in gram_copies:
        copy.wait()
    solve_rows = []
    for tile, total in enumerate(gathered(gram_own, gram_got)):
        sums = jnp.sum(total, axis=1, keepdims=True)
        centre = ((block + tile - 1).astype(F32) * COLS + COLS // 2) / SLAB_COLS - 0.5
        g00, g01, g02 = sums[0:1] + 1.0, sums[1:2], sums[2:3] - centre
        g11, g12, g22 = sums[3:4] + 1.0, sums[4:5], sums[5:6] + (1.0 + centre * centre)
        c00, c01, c02 = g11 * g22 - g12 * g12, g02 * g12 - g01 * g22, g01 * g12 - g02 * g11
        c11, c12, c22 = g00 * g22 - g02 * g02, g01 * g02 - g00 * g12, g00 * g11 - g01 * g01
        determinant = g00 * c00 + g01 * c01 + g02 * c02
        _, along_u, along_v = basis_rows[tile]
        member = lanes([members[tile][0:1], members[tile][1:2]])
        for first, second, third in ((c00, c01, c02), (c01, c11, c12), (c02, c12, c22)):
            solve_rows.append(
                member * ((first + second * along_u + third * along_v) / determinant)
            )
        solve_rows.append(jnp.zeros((1, PIXELS), F32))
    solve_rows.append(jnp.zeros((4, PIXELS), F32))
    solve_v[...] = jnp.concatenate(solve_rows, axis=0)
    solve_store = pltpu.make_async_copy(solve_v, solve_out, store_sem.at[0])
    solve_store.start()
    weight_rows = []
    for tile in range(3):
        weight = lanes([weights[tile][0:1], weights[tile][1:2]])
        weight_rows += [weight * row for row in basis_rows[tile]]
        weight_rows.append(jnp.zeros((1, PIXELS), F32))
    weight_rows.append(jnp.zeros((4, PIXELS), F32))
    moment_weights = jnp.concatenate(weight_rows, axis=0).astype(BF16)
    coh_lanes = lanes([coh[0:1], coh[1:2]])

    small[4].wait()
    pltpu.make_async_copy(
        stacked.at[pl.ds(0, IFGS - OWN_IFGS)], stacked.at[pl.ds(0, IFGS - OWN_IFGS)], phase_recv
    ).wait()

    wide[...] = stacked.reshape(ROWS * IFGS, COLS)[...].astype(F32)
    for row in range(ROWS):
        values[:, COLS * row : COLS * row + COLS] = wide[pl.ds(row, IFGS, stride=ROWS), :]
    values_half[...] = values[...].astype(BF16)
    series[...] = dot(gain_hi[...], values_half[...]) + dot(gain_lo[...], values_half[...])
    for sweep in range(REWEIGHTS):
        series_hi[0:DATE_ROWS, :], series_lo[0:DATE_ROWS, :] = split(series[...])
        residual = values[...] - (
            dot(incidence[...], series_hi[...]) + dot(incidence[...], series_lo[...])
        )
        square = residual * residual
        scale = jnp.sum(square, axis=0, keepdims=True) * (1.0 / IFGS) + 1e-6
        ratio = scale / (square + scale)
        pull_hi[...], pull_lo[...] = split(coh_lanes * (ratio * ratio) * residual)
        series[...] = series[...] + (
            dot(gain_hi[...], pull_hi[...])
            + dot(gain_hi[...], pull_lo[...])
            + dot(gain_lo[...], pull_hi[...])
        )
    series_hi[0:DATE_ROWS, :], series_lo[0:DATE_ROWS, :] = split(series[...])
    series_store = pltpu.make_async_copy(series, series_out, store_sem.at[1])
    series_store.start()

    over_pixels = (((1,), (1,)), ((), ()))
    moments = lax.dot_general(
        moment_weights, series_hi[...], over_pixels, preferred_element_type=F32
    ) + lax.dot_general(moment_weights, series_lo[...], over_pixels, preferred_element_type=F32)
    for tile in range(3):
        moments_own[tile] = moments[4 * tile : 4 * tile + 4, :]
    moment_copies = trade(moments_own, moments_got, moment_send, moment_recv)
    for copy in moment_copies:
        copy.wait()
    moments_all[...] = jnp.concatenate(
        gathered(moments_own, moments_got) + [jnp.zeros((4, DATE_LANES), F32)], axis=0
    )
    moments_store = pltpu.make_async_copy(moments_all, moments_out, store_sem.at[2])
    moments_store.start()

    pltpu.make_async_copy(
        phases.at[:, :, pl.ds(COLS, (STACK - 1) * COLS)],
        phases.at[:, :, pl.ds(COLS, (STACK - 1) * COLS)],
        phase_send,
    ).wait()
    solve_store.wait()
    series_store.wait()
    moments_store.wait()


def deramp_kernel(series, moments, solve, out):
    over_terms = (((0,), (0,)), ((), ()))
    m_hi, m_lo = split(moments[...])
    s_hi, s_lo = split(solve[...])
    plane = lax.dot_general(
        jnp.concatenate([m_hi, m_lo, m_hi], axis=0),
        jnp.concatenate([s_hi, s_hi, s_lo], axis=0),
        over_terms,
        preferred_element_type=F32,
    )
    flat = series[0:DATES, :] - plane[0:DATES, :]
    out_rows = out.reshape(DATES * ROWS, COLS)
    for row in range(ROWS):
        out_rows[pl.ds(row, DATES, stride=ROWS), :] = flat[:, COLS * row : COLS * row + COLS]


def local(phases, ifg_pairs, preconditioner, coherence, geo_tiles):
    anywhere = pl.BlockSpec(memory_space=pl.ANY)
    vmem = pl.BlockSpec(memory_space=pltpu.VMEM)
    dma = pltpu.SemaphoreType.DMA
    series, moments, solve = pl.pallas_call(
        invert_kernel,
        out_shape=(
            jax.ShapeDtypeStruct((DATE_ROWS, PIXELS), F32),
            jax.ShapeDtypeStruct((16, DATE_LANES), F32),
            jax.ShapeDtypeStruct((16, PIXELS), F32),
        ),
        in_specs=[anywhere] * 5,
        out_specs=(anywhere,) * 3,
        scratch_shapes=[
            pltpu.VMEM((IFGS, ROWS, COLS), BF16),
            pltpu.VMEM((ROWS * IFGS, COLS), F32),
            pltpu.VMEM((IFGS, PIXELS), F32),
            pltpu.VMEM((IFGS, PIXELS), BF16),
            pltpu.VMEM((2, IFGS), jnp.int32),
            pltpu.VMEM((DATES, DATES), F32),
            pltpu.VMEM((DATE_ROWS, DATE_LANES), F32),
            pltpu.VMEM((ROWS, COLS), jnp.int32),
            pltpu.VMEM((ROWS, COLS), jnp.int32),
            pltpu.VMEM((IFGS, DATE_LANES), BF16),
            pltpu.VMEM((DATE_LANES, IFGS), BF16),
            pltpu.VMEM((DATE_ROWS, IFGS), BF16),
            pltpu.VMEM((DATE_ROWS, IFGS), BF16),
            pltpu.VMEM((DATE_ROWS, PIXELS), F32),
            pltpu.VMEM((DATE_LANES, PIXELS), BF16),
            pltpu.VMEM((DATE_LANES, PIXELS), BF16),
            pltpu.VMEM((IFGS, PIXELS), BF16),
            pltpu.VMEM((IFGS, PIXELS), BF16),
            pltpu.VMEM((3, 8, COLS), F32),
            pltpu.VMEM((2, 5, 3, 8, COLS), F32),
            pltpu.VMEM((3, 4, DATE_LANES), F32),
            pltpu.VMEM((2, 5, 3, 4, DATE_LANES), F32),
            pltpu.VMEM((16, DATE_LANES), F32),
            pltpu.VMEM((16, PIXELS), F32),
            dma((5,)),
            dma((3,)),
            dma,
            dma,
            dma((2, 5)),
            dma((2, 5)),
            dma((2, 5)),
            dma((2, 5)),
        ],
        compiler_params=pltpu.CompilerParams(
            collective_id=0, has_side_effects=True, vmem_limit_bytes=56 * 2**20
        ),
    )(phases, ifg_pairs.T, preconditioner, coherence, geo_tiles)
    return pl.pallas_call(
        deramp_kernel,
        out_shape=jax.ShapeDtypeStruct((DATES, ROWS, COLS), F32),
        in_specs=[vmem] * 3,
        out_specs=vmem,
    )(series, moments, solve)


def solution(mesh):
    return jax.shard_map(
        local,
        mesh=mesh,
        in_specs=(
            P("stack", "azimuth", "range"),
            P(),
            P(),
            P("azimuth", ("range", "stack")),
            P("azimuth", ("range", "stack")),
        ),
        out_specs=P(None, "azimuth", ("range", "stack")),
        check_vma=False,
    )
```

```python
import functools

import jax
import jax.numpy as jnp
from jax import lax
from jax.experimental import pallas as pl
from jax.experimental.pallas import tpu as pltpu
from jax.sharding import PartitionSpec as P

MESH = pl.DeviceIdType.MESH
F32 = jnp.float32
BF16 = jnp.bfloat16
REWEIGHTS = 2
IFGS = 1152
DATES = 600
DATE_ROWS = 608
DATE_LANES = 640
COLS = 128
ROWS = 2
PIXELS = ROWS * COLS
SLAB_ROWS = 4
SLAB_COLS = 32768
STACK = 128
SIDE = 8
OWN_IFGS = IFGS // STACK
BLOCKS = SLAB_COLS // COLS
REACH = (-2, -1, 0, 1, 2)
IFG_PARTS = (slice(0, 512), slice(512, 1152))


def split(value):
    high = value.astype(BF16)
    return high, (value - high.astype(F32)).astype(BF16)


def dot(left, right):
    return jnp.dot(left, right, preferred_element_type=F32)


def ring_hops(step):
    return min(step % SIDE, -step % SIDE)


def far_first():
    steps = [(dz, dy, dc) for dz in range(SIDE) for dy in range(SIDE) for dc in range(2)]
    steps.remove((0, 0, 0))
    return sorted(steps, key=lambda step: -ring_hops(step[0]) - ring_hops(step[1]))


def invert_kernel(
    phases,
    pairs,
    precond,
    coherence,
    tiles,
    series_out,
    moments_out,
    solve_out,
    stacked,
    wide,
    values,
    values_half,
    pairs_v,
    precond_v,
    precond_pad,
    coherence_v,
    tiles_v,
    incidence,
    incidence_t,
    gain_hi,
    gain_lo,
    series,
    halves,
    residual,
    pull_hi,
    pull_lo,
    gram_own,
    gram_got,
    moments_own,
    moments_got,
    moments_all,
    solve_v,
    load_sem,
    store_sem,
    phase_send,
    phase_recv,
    gram_send,
    gram_recv,
    moment_send,
    moment_recv,
):
    me = lax.axis_index("stack")
    azimuth = lax.axis_index("azimuth")
    block = lax.axis_index("range") * STACK + me
    z, y, core = me // (2 * SIDE), lax.rem(me // 2, SIDE), lax.rem(me, 2)

    def peer(reach, other):
        there = lax.rem(block + reach + BLOCKS, BLOCKS)
        return {
            "stack": lax.rem(there, STACK),
            "azimuth": (1 - azimuth) if other else azimuth,
            "range": there // STACK,
        }

    group = [(reach, other) for other in (0, 1) for reach in REACH if reach or other]

    barrier = pltpu.get_barrier_semaphore()

    def neighbour(dz, dy, dc):
        return (
            lax.rem(z + dz, SIDE) * (2 * SIDE) + lax.rem(y + dy, SIDE) * 2 + lax.rem(core + dc, 2)
        )

    for step in far_first():
        pl.semaphore_signal(
            barrier, inc=1, device_id={"stack": neighbour(*step)}, device_id_type=MESH
        )
    for reach, other in group:
        pl.semaphore_signal(barrier, inc=1, device_id=peer(reach, other), device_id_type=MESH)

    small = [
        pltpu.make_async_copy(coherence, coherence_v, load_sem.at[0]),
        pltpu.make_async_copy(tiles, tiles_v, load_sem.at[1]),
        pltpu.make_async_copy(pairs, pairs_v, load_sem.at[2]),
        pltpu.make_async_copy(precond, precond_v, load_sem.at[3]),
        pltpu.make_async_copy(
            phases.at[:, :, pl.ds(pl.multiple_of(me * COLS, COLS), COLS)],
            stacked.at[pl.ds(OWN_IFGS * me, OWN_IFGS)],
            load_sem.at[4],
        ),
    ]
    for copy in small:
        copy.start()

    pl.semaphore_wait(barrier, STACK - 1 + len(group))

    for step in far_first():
        there = neighbour(*step)
        pltpu.make_async_remote_copy(
            src_ref=phases.at[:, :, pl.ds(pl.multiple_of(there * COLS, COLS), COLS)],
            dst_ref=stacked.at[pl.ds(OWN_IFGS * me, OWN_IFGS)],
            send_sem=phase_send,
            recv_sem=phase_recv,
            device_id={"stack": there},
            device_id_type=MESH,
        ).start()

    small[0].wait()
    small[1].wait()
    coh = coherence_v[...].astype(F32)
    tile_ids = tiles_v[...]
    column = lax.broadcasted_iota(jnp.int32, (1, COLS), 1).astype(F32)
    row_u = [
        ((azimuth * ROWS + row).astype(F32) + 0.5) / SLAB_ROWS - 0.5 for row in range(ROWS)
    ]
    offset_v = [(column - (63.5 + COLS * tile)) / SLAB_COLS for tile in (-1, 0, 1)]
    members = [(tile_ids == block + tile).astype(F32) for tile in (-1, 0, 1)]
    weights = [coh * member for member in members]

    def lanes(pieces):
        return jnp.concatenate(pieces, axis=1)

    basis_rows = []
    for tile in range(3):
        ones = jnp.ones((1, COLS), F32)
        basis_rows.append(
            [
                lanes([ones, ones]),
                lanes([ones * row_u[0], ones * row_u[1]]),
                lanes([offset_v[tile], offset_v[tile]]),
            ]
        )
        w0, w1 = weights[tile][0:1], weights[tile][1:2]
        dv = offset_v[tile]
        both, lean = w0 + w1, w0 * row_u[0] + w1 * row_u[1]
        gram_own[tile] = jnp.concatenate(
            [
                both,
                lean,
                both * dv,
                w0 * (row_u[0] * row_u[0]) + w1 * (row_u[1] * row_u[1]),
                lean * dv,
                both * dv * dv,
                jnp.zeros((2, COLS), F32),
            ],
            axis=0,
        )

    def trade(own, got, unit, send_sem, recv_sem):
        copies = []
        for reach, other in group:
            first, last = max(0, reach), min(3, 3 + reach)
            copies.append(
                pltpu.make_async_remote_copy(
                    src_ref=own.at[pl.ds(unit * first, unit * (last - first))],
                    dst_ref=got.at[
                        other, reach + 2, pl.ds(unit * (first - reach), unit * (last - first))
                    ],
                    send_sem=send_sem.at[other, reach + 2],
                    recv_sem=recv_sem.at[other, reach + 2],
                    device_id=peer(reach, other),
                    device_id_type=MESH,
                )
            )
        for copy in copies:
            copy.start()
        return copies

    def gathered(own, got, unit):
        totals = []
        for place in range(3 * unit):
            total = own[place]
            for reach, other in group:
                if max(0, reach) - reach <= place // unit < min(3, 3 + reach) - reach:
                    total = total + got[other, reach + 2, place]
            totals.append(total)
        return totals

    gram_copies = trade(gram_own, gram_got, 1, gram_send, gram_recv)

    small[2].wait()
    earlier, later = pairs_v[0:1, :], pairs_v[1:2, :]
    date_rows = lax.broadcasted_iota(jnp.int32, (DATE_LANES, IFGS), 0)
    incidence_t[...] = (
        jnp.where(later == date_rows, 1.0, 0.0) - jnp.where(earlier == date_rows, 1.0, 0.0)
    ).astype(BF16)
    later_col = jnp.broadcast_to(later.astype(F32), (COLS, IFGS)).T
    earlier_col = jnp.broadcast_to(earlier.astype(F32), (COLS, IFGS)).T
    for part in range(DATE_LANES // 128):
        date_lanes = (
            lax.broadcasted_iota(jnp.int32, (IFGS, 128), 1) + 128 * part
        ).astype(F32)
        columns = (
            jnp.where(later_col == date_lanes, 1.0, 0.0)
            - jnp.where(earlier_col == date_lanes, 1.0, 0.0)
        ).astype(BF16)
        incidence[:, 128 * part : 128 * part + 128] = columns
        incidence[:, DATE_LANES + 128 * part : DATE_LANES + 128 * part + 128] = columns
    precond_pad[...] = jnp.zeros((DATE_ROWS, DATE_LANES), F32)
    small[3].wait()
    precond_pad[0:DATES, 0:DATES] = precond_v[...]
    first_hi, first_lo = split(precond_pad[...])
    gain = dot(first_hi, incidence_t[...]) + dot(first_lo, incidence_t[...])
    gain_hi[...], gain_lo[...] = split(gain)
    halves[...] = jnp.zeros((2 * DATE_LANES, PIXELS), BF16)

    for copy in gram_copies:
        copy.wait()
    solve_rows = []
    for tile, total in enumerate(gathered(gram_own, gram_got, 1)):
        sums = jnp.sum(total, axis=1, keepdims=True)
        centre = ((block + tile - 1).astype(F32) * COLS + COLS // 2) / SLAB_COLS - 0.5
        g00, g01, g02 = sums[0:1] + 1.0, sums[1:2], sums[2:3] - centre
        g11, g12, g22 = sums[3:4] + 1.0, sums[4:5], sums[5:6] + (1.0 + centre * centre)
        c00, c01, c02 = g11 * g22 - g12 * g12, g02 * g12 - g01 * g22, g01 * g12 - g02 * g11
        c11, c12, c22 = g00 * g22 - g02 * g02, g01 * g02 - g00 * g12, g00 * g11 - g01 * g01
        determinant = g00 * c00 + g01 * c01 + g02 * c02
        _, along_u, along_v = basis_rows[tile]
        member = lanes([members[tile][0:1], members[tile][1:2]])
        for first, second, third in ((c00, c01, c02), (c01, c11, c12), (c02, c12, c22)):
            solve_rows.append(
                member * ((first + second * along_u + third * along_v) / determinant)
            )
    solve_rows.append(jnp.zeros((7, PIXELS), F32))
    solve_v[...] = jnp.concatenate(solve_rows, axis=0)
    solve_store = pltpu.make_async_copy(solve_v, solve_out, store_sem.at[0])
    solve_store.start()
    weight_rows = []
    for tile in range(3):
        weight = lanes([weights[tile][0:1], weights[tile][1:2]])
        weight_rows += [weight * row for row in basis_rows[tile]]
        weight_rows.append(jnp.zeros((1, PIXELS), F32))
    weight_rows.append(jnp.zeros((4, PIXELS), F32))
    moment_weights = jnp.concatenate(weight_rows, axis=0).astype(BF16)
    coh_lanes = lanes([coh[0:1], coh[1:2]])

    small[4].wait()
    pltpu.make_async_copy(
        stacked.at[pl.ds(0, IFGS - OWN_IFGS)], stacked.at[pl.ds(0, IFGS - OWN_IFGS)], phase_recv
    ).wait()

    flat = stacked.reshape(ROWS * IFGS, COLS)
    total = jnp.zeros((DATE_ROWS, PIXELS), F32)
    for part in IFG_PARTS:
        first = ROWS * part.start
        wide[first : ROWS * part.stop, :] = flat[first : ROWS * part.stop, :].astype(F32)
        for row in range(ROWS):
            lane = slice(COLS * row, COLS * row + COLS)
            column = wide[pl.ds(first + row, part.stop - part.start, stride=ROWS), :]
            values[part, lane] = column
            values_half[part, lane] = column.astype(BF16)
        total = total + dot(gain_hi[:, part], values_half[part, :])
        total = total + dot(gain_lo[:, part], values_half[part, :])
    series[...] = total

    def halve():
        high, low = split(series[...])
        halves[0:DATE_ROWS, :] = high
        halves[DATE_LANES : DATE_LANES + DATE_ROWS, :] = low

    for sweep in range(REWEIGHTS):
        halve()
        squares = jnp.zeros((8, PIXELS), F32)
        for part in range(2):
            rows = slice(IFGS // 2 * part, IFGS // 2 * (part + 1))
            misfit = values[rows, :] - dot(incidence[rows, :], halves[...])
            residual[rows, :] = misfit
            squares = squares + jnp.sum((misfit * misfit).reshape(IFGS // 16, 8, PIXELS), axis=0)
        scale = jnp.sum(squares, axis=0, keepdims=True) * (1.0 / IFGS) + 1e-6
        coherent_scale = coh_lanes * scale
        total = series[...]
        for part in IFG_PARTS:
            misfit = residual[part, :]
            ratio = coherent_scale / (misfit * misfit + scale)
            pull_hi[part, :], pull_lo[part, :] = split((ratio * ratio) * misfit)
            total = total + dot(gain_hi[:, part], pull_hi[part, :])
            total = total + dot(gain_lo[:, part], pull_hi[part, :])
            total = total + dot(gain_hi[:, part], pull_lo[part, :])
        series[...] = total
    halve()
    series_store = pltpu.make_async_copy(series, series_out, store_sem.at[1])
    series_store.start()

    over_pixels = (((1,), (1,)), ((), ()))
    moments = lax.dot_general(
        moment_weights, halves[0:DATE_LANES, :], over_pixels, preferred_element_type=F32
    ) + lax.dot_general(
        moment_weights, halves[DATE_LANES:, :], over_pixels, preferred_element_type=F32
    )
    for tile in range(3):
        for term in range(3):
            moments_own[3 * tile + term] = moments[4 * tile + term : 4 * tile + term + 1, :]
    moment_copies = trade(moments_own, moments_got, 3, moment_send, moment_recv)
    for copy in moment_copies:
        copy.wait()
    moments_all[...] = jnp.concatenate(
        gathered(moments_own, moments_got, 3) + [jnp.zeros((7, DATE_LANES), F32)], axis=0
    )
    moments_store = pltpu.make_async_copy(moments_all, moments_out, store_sem.at[2])
    moments_store.start()

    pltpu.make_async_copy(
        phases.at[:, :, pl.ds(COLS, (STACK - 1) * COLS)],
        phases.at[:, :, pl.ds(COLS, (STACK - 1) * COLS)],
        phase_send,
    ).wait()
    solve_store.wait()
    series_store.wait()
    moments_store.wait()


def deramp_kernel(series_in, moments_in, solve_in, out, series, moments, solve, load_sem):
    copies = [
        pltpu.make_async_copy(source, target, load_sem.at[place])
        for place, (source, target) in enumerate(
            ((moments_in, moments), (solve_in, solve), (series_in, series))
        )
    ]
    for copy in copies:
        copy.start()
    for copy in copies:
        copy.wait()
    over_terms = (((0,), (0,)), ((), ()))
    m_hi, m_lo = split(moments[...])
    s_hi, s_lo = split(solve[...])
    plane = lax.dot_general(
        jnp.concatenate([m_hi, m_lo, m_hi], axis=0),
        jnp.concatenate([s_hi, s_hi, s_lo], axis=0),
        over_terms,
        preferred_element_type=F32,
    )
    flat = series[0:DATES, :] - plane[0:DATES, :]
    out_rows = out.reshape(DATES * ROWS, COLS)
    for row in range(ROWS):
        out_rows[pl.ds(row, DATES, stride=ROWS), :] = flat[:, COLS * row : COLS * row + COLS]


def local(phases, ifg_pairs, preconditioner, coherence, geo_tiles):
    anywhere = pl.BlockSpec(memory_space=pl.ANY)
    hbm = pl.BlockSpec(memory_space=pltpu.HBM)
    vmem = pl.BlockSpec(memory_space=pltpu.VMEM)
    dma = pltpu.SemaphoreType.DMA
    series, moments, solve = pl.pallas_call(
        invert_kernel,
        out_shape=(
            jax.ShapeDtypeStruct((DATE_ROWS, PIXELS), F32),
            jax.ShapeDtypeStruct((16, DATE_LANES), F32),
            jax.ShapeDtypeStruct((16, PIXELS), F32),
        ),
        in_specs=[hbm] * 5,
        out_specs=(anywhere,) * 3,
        scratch_shapes=[
            pltpu.VMEM((IFGS, ROWS, COLS), BF16),
            pltpu.VMEM((ROWS * IFGS, COLS), F32),
            pltpu.VMEM((IFGS, PIXELS), F32),
            pltpu.VMEM((IFGS, PIXELS), BF16),
            pltpu.VMEM((2, IFGS), jnp.int32),
            pltpu.VMEM((DATES, DATES), F32),
            pltpu.VMEM((DATE_ROWS, DATE_LANES), F32),
            pltpu.VMEM((ROWS, COLS), jnp.int32),
            pltpu.VMEM((ROWS, COLS), jnp.int32),
            pltpu.VMEM((IFGS, 2 * DATE_LANES), BF16),
            pltpu.VMEM((DATE_LANES, IFGS), BF16),
            pltpu.VMEM((DATE_ROWS, IFGS), BF16),
            pltpu.VMEM((DATE_ROWS, IFGS), BF16),
            pltpu.VMEM((DATE_ROWS, PIXELS), F32),
            pltpu.VMEM((2 * DATE_LANES, PIXELS), BF16),
            pltpu.VMEM((IFGS, PIXELS), F32),
            pltpu.VMEM((IFGS, PIXELS), BF16),
            pltpu.VMEM((IFGS, PIXELS), BF16),
            pltpu.VMEM((3, 8, COLS), F32),
            pltpu.VMEM((2, 5, 3, 8, COLS), F32),
            pltpu.VMEM((9, 1, DATE_LANES), F32),
            pltpu.VMEM((2, 5, 9, 1, DATE_LANES), F32),
            pltpu.VMEM((16, DATE_LANES), F32),
            pltpu.VMEM((16, PIXELS), F32),
            dma((5,)),
            dma((3,)),
            dma,
            dma,
            dma((2, 5)),
            dma((2, 5)),
            dma((2, 5)),
            dma((2, 5)),
        ],
        compiler_params=pltpu.CompilerParams(
            collective_id=0, has_side_effects=True, vmem_limit_bytes=40 * 2**20
        ),
    )(*(
        pltpu.with_memory_space_constraint(array, pltpu.HBM)
        for array in (phases, ifg_pairs.T, preconditioner, coherence, geo_tiles)
    ))
    return pl.pallas_call(
        deramp_kernel,
        out_shape=jax.ShapeDtypeStruct((DATES, ROWS, COLS), F32),
        in_specs=[anywhere] * 3,
        out_specs=vmem,
        scratch_shapes=[
            pltpu.VMEM((DATE_ROWS, PIXELS), F32),
            pltpu.VMEM((16, DATE_LANES), F32),
            pltpu.VMEM((16, PIXELS), F32),
            dma((3,)),
        ],
        compiler_params=pltpu.CompilerParams(vmem_limit_bytes=16 * 2**20),
    )(series, moments, solve)


def solution(mesh):
    return jax.shard_map(
        local,
        mesh=mesh,
        in_specs=(
            P("stack", "azimuth", "range"),
            P(),
            P(),
            P("azimuth", ("range", "stack")),
            P("azimuth", ("range", "stack")),
        ),
        out_specs=P(None, "azimuth", ("range", "stack")),
        check_vma=False,
    )
```
